32 devices in a mesh: week: 8 (over z, y), seg: 4 (over x, core).
Axes of the slice: x: 2, y: 2, z: 4, core: 2. Of those that a mesh axis runs over, the one named last changes fastest.
Arguments:
- right_side: float32 [48, 4, 16384], P(None, 'seg', 'week'), may hold values from -6 to 6
- jacobians: bfloat16 [64, 256, 4096], P('week', None, 'seg'), may hold values from -0.1875 to 0.1875
- week_blocks: int32 [64, 32], P('week', 'seg'), may hold values from 0 to 127, as said below
- block_kind: int32 [4, 128], P('seg', 'week'), may hold values from 0 to 7
- diagonal_table: float32 [8, 128, 128], replicated, as said below
- precond_table: float32 [8, 128, 128], replicated, as said below
Outputs:
- solution_field: float32 [48, 4, 16384], P(None, 'seg', 'week')
- residual: float32 [48, 4, 16384], P(None, 'seg', 'week')
The draws below stay inside these ranges and needn't reach their ends.
Inputs may be any that keep to these rules, and one draw needn't show every extreme that they name: `week_blocks`: entry j of a week's row names a block of segment j // 8 by its number within that segment; the 8 entries of one segment in one row are distinct. `diagonal_table`: each block is symmetric positive definite. `precond_table`: each block is symmetric positive definite.
All inputs are finite; a program needn't handle non-finite values.
Results may differ from the reference program's by a relative error of at most 0.035.
Values may be sent and summed in bfloat16 or wider, within the bound.
A program may use at most 128 MiB of HBM per device.

```python
import math
import jax
import jax.numpy as jnp
from jax import lax

P_SIZE = 65536
S = 4096
R = 256
BLK = 128
KINDS = 8
ITERS = 4
NRHS = 48
W_DEV = 8
WEEKS = 64
SEGS = 4
SEG_LEN = 16384
SUB_SEG = 1024
KB = 8
BLOCKS_SEG = 128


def draw_week_blocks(key, part):
    scores = jax.random.randint(key, (WEEKS, SEGS, BLOCKS_SEG), 0, 1 << 20) * BLOCKS_SEG + jnp.arange(BLOCKS_SEG, dtype=jnp.int32)
    picked = jnp.argsort(scores, axis=-1, stable=True)[:, :, :KB]
    return picked.reshape(WEEKS, SEGS * KB).astype(jnp.int32)


def symmetric_blocks(key, lower, upper):
    key_one, key_two = jax.random.split(key)
    diagonal_part = jax.random.uniform(key_one, (KINDS, BLK), jnp.float32, lower, upper)
    random_part = jax.random.normal(key_two, (KINDS, BLK, BLK), jnp.float32) * (0.5 / math.sqrt(2.0 * BLK))
    symmetric = random_part + jnp.swapaxes(random_part, 1, 2)
    return symmetric + diagonal_part[:, :, None] * jnp.eye(BLK, dtype=jnp.float32)


def draw_diagonal_table(key, part):
    return symmetric_blocks(jax.random.fold_in(key, 11), 1.5, 2.5)


def draw_precond_table(key, part):
    return symmetric_blocks(jax.random.fold_in(key, 23), 1.5, 3.0)


def place_ends(drawn, key, smallest, high):
    place = [jax.random.randint(jax.random.fold_in(key, axis), (), 0, length) for axis, length in enumerate(drawn.shape)]
    main_axis = drawn.shape.index(max(drawn.shape))
    neighbour = place[:main_axis] + [(place[main_axis] + 1) % drawn.shape[main_axis]] + place[main_axis + 1:]
    return drawn.at[tuple(place)].set(smallest).at[tuple(neighbour)].set(high)


def steps_of(key, extent, cuts, smallest, high):
    factor_of, own = 1.0, jax.random.fold_in(key, 6)
    for position, parts in cuts:
        steps = jnp.exp(jax.random.uniform(jax.random.fold_in(own, position), (parts,), jnp.float32, smallest / len(cuts), high / len(cuts)))
        factor_of = factor_of * jnp.repeat(steps, extent[position] // parts).reshape([-1 if axis == position else 1 for axis in range(len(extent))])
    return factor_of


def bell_draw(own_key, extent, deviation, reach, cuts=(), kind=jnp.bfloat16):
    values = jax.random.normal(own_key, extent, jnp.float32) * deviation
    if len(cuts) > 0:
        values = steps_of(own_key, extent, cuts, -0.22, 0.18) * values
    return jnp.clip(values, min=-reach, max=reach).astype(kind)


def setup_inputs(seed: int = 0) -> dict:
    keys = jax.random.split(jax.random.key(seed), 7)
    return {
        "right_side": bell_draw(keys[0], (NRHS, SEGS, SEG_LEN), 1.0, 6.0, ((1, 4), (2, 8)), jnp.float32),
        "jacobians": bell_draw(keys[1], (WEEKS, R, S), (max(R * WEEKS * SUB_SEG // SEG_LEN, 1)) ** -0.5, 0.1875, ((0, 8), (2, 4))),
        "week_blocks": draw_week_blocks(jax.random.fold_in(keys[6], 71), 0),
        "block_kind": place_ends(jax.random.randint(keys[3], (SEGS, BLOCKS_SEG), 0, KINDS), jax.random.fold_in(keys[3], 1), 0, KINDS - 1).astype(jnp.int32),
        "diagonal_table": draw_diagonal_table(jax.random.fold_in(keys[6], 71), 0),
        "precond_table": draw_precond_table(jax.random.fold_in(keys[6], 71), 0),
    }


def block_apply(vector, blocks):
    shaped = vector.reshape(vector.shape[0], blocks.shape[0], blocks.shape[1])
    result = jnp.einsum("kbc,bcd->kbd", shaped, blocks, precision=lax.Precision.HIGHEST)
    return result.reshape(vector.shape[0], -1)


def reference(right_side, jacobians, week_blocks, block_kind, diagonal_table, precond_table):
    right = right_side.reshape(NRHS, P_SIZE)
    kinds = block_kind.reshape(-1)
    diag_blocks = diagonal_table[kinds]
    pre_blocks = precond_table[kinds]
    column = jnp.arange(S, dtype=jnp.int32)
    columns = ((column // SUB_SEG) * SEG_LEN + week_blocks[:, column // BLK] * BLK + column % BLK).astype(jnp.int32)
    stacked = jacobians.reshape(WEEKS // W_DEV, W_DEV, R, S)
    index_blocks = columns.reshape(WEEKS // W_DEV, W_DEV, S)

    def operate(direction):
        rounded = direction.astype(jnp.bfloat16).astype(jnp.float32)

        def add_weeks(total_acc, pieces):
            factor, cols_here = pieces
            factor32 = factor.astype(jnp.float32)
            picked = rounded[:, cols_here]
            projected = jnp.einsum("wrc,kwc->kwr", factor32, picked, precision=lax.Precision.HIGHEST)
            projected = lax.optimization_barrier(projected.astype(jnp.bfloat16)).astype(jnp.float32)
            spread = jnp.einsum("wrc,kwr->kwc", factor32, projected, precision=lax.Precision.HIGHEST)
            return total_acc.at[:, cols_here].add(spread), None

        image, _ = lax.scan(add_weeks, jnp.zeros((NRHS, P_SIZE), jnp.float32), (stacked, index_blocks))
        return image + block_apply(direction, diag_blocks)

    def inner(first_vec, second_vec):
        return jnp.sum(first_vec * second_vec, axis=1)

    solution = jnp.zeros((NRHS, P_SIZE), jnp.float32)
    residual = right
    precond = block_apply(residual, pre_blocks)
    direction = precond
    rz_now = inner(residual, precond)
    for step in range(ITERS):
        image = operate(direction)
        step_size = rz_now / inner(direction, image)
        solution = solution + step_size[:, None] * direction
        residual = residual - step_size[:, None] * image
        if step + 1 < ITERS:
            precond = block_apply(residual, pre_blocks)
            rz_next = inner(residual, precond)
            direction = precond + (rz_next / rz_now)[:, None] * direction
            rz_now = rz_next
    return solution.reshape(NRHS, SEGS, SEG_LEN), residual.reshape(NRHS, SEGS, SEG_LEN)
```

```python
import jax
import jax.numpy as jnp
from jax import lax
from jax.sharding import PartitionSpec as P

ITERS = 4


def block_apply(vector, blocks):
    return jnp.einsum("bkc,bcd->bkd", vector, blocks, precision=lax.Precision.HIGHEST)


def per_device(right_side, jacobians, week_blocks, block_kind, diagonal_table, precond_table):
    rhs_count = right_side.shape[0]
    weeks, rank, columns = jacobians.shape
    picks = week_blocks.shape[1]
    width = columns // picks
    own_blocks = right_side.shape[2] // width
    block_count = own_blocks * lax.axis_size("week")
    kinds = block_kind[0]
    diag_blocks = diagonal_table[kinds]
    pre_blocks = precond_table[kinds]
    flat_ids = week_blocks.reshape(-1)
    onehot = (
        jnp.arange(block_count, dtype=jnp.int32)[:, None] == flat_ids[None, :]
    ).astype(jnp.bfloat16)
    factors = jacobians.reshape(weeks, rank, picks, width)

    def inner(first_vec, second_vec):
        return lax.psum(jnp.sum(first_vec * second_vec, axis=(0, 2)), ("week", "seg"))

    def operate(direction):
        whole = lax.all_gather(direction.astype(jnp.bfloat16), "week", axis=0, tiled=True)
        picked = jnp.take(whole, flat_ids, axis=0).reshape(weeks, picks, rhs_count, width)
        partial_value = jnp.einsum(
            "wrjc,wjkc->wkr", factors, picked, preferred_element_type=jnp.float32
        )
        summed = lax.psum(partial_value.astype(jnp.bfloat16), "seg")
        spread = jnp.einsum(
            "wrjc,wkr->wjkc", factors, summed, preferred_element_type=jnp.float32
        ).astype(jnp.bfloat16)
        placed = jnp.einsum(
            "sb,bkc->skc",
            onehot,
            spread.reshape(weeks * picks, rhs_count, width),
            preferred_element_type=jnp.float32,
        ).astype(jnp.bfloat16)
        image = lax.psum_scatter(placed, "week", scatter_dimension=0, tiled=True)
        return image.astype(jnp.float32) + block_apply(direction, diag_blocks)

    residual = right_side.reshape(rhs_count, own_blocks, width).transpose(1, 0, 2)
    solution = jnp.zeros_like(residual)
    precond = block_apply(residual, pre_blocks)
    direction = precond
    rz_now = inner(residual, precond)
    for step in range(ITERS):
        image = operate(direction)
        step_size = (rz_now / inner(direction, image))[None, :, None]
        solution = solution + step_size * direction
        residual = residual - step_size * image
        if step + 1 < ITERS:
            precond = block_apply(residual, pre_blocks)
            rz_next = inner(residual, precond)
            direction = precond + (rz_next / rz_now)[None, :, None] * direction
            rz_now = rz_next

    def leave(value):
        return value.transpose(1, 0, 2).reshape(right_side.shape)

    return (leave(solution), leave(residual))


def solution(mesh):
    placed = (
        P(None, "seg", "week"),
        P("week", None, "seg"),
        P("week", "seg"),
        P("seg", "week"),
        P(),
        P(),
    )
    return jax.shard_map(
        per_device,
        mesh=mesh,
        in_specs=placed,
        out_specs=(P(None, "seg", "week"), P(None, "seg", "week")),
        check_vma=False,
    )
```

```python
import functools

import jax
import jax.numpy as jnp
from jax import lax
from jax.experimental import pallas as pl
from jax.experimental.pallas import tpu as pltpu
from jax.sharding import PartitionSpec as P

ITERS = 4
LANES = 128
MESH = pl.DeviceIdType.MESH
HIGHEST = lax.Precision.HIGHEST


def dot32(left, right):
    return jnp.dot(left, right, precision=HIGHEST, preferred_element_type=jnp.float32)


def kernel(
    nw, ns, wb_ref, inv_ref, kind_ref, right_ref, jac_ref, dtab_ref, mtab_ref, x_out, r_out,
    zfull, part, segr, ownp, proj, pbuf, spread, tbuf, rsr, own, x_s, r_s, z_s, p_s, dz_s, dp_s,
    pad, rz_old, rzw, rzs, paw, pas,
    ag_sem, sg_sem, pb_sem, rs_sem, rzw_sem, rzs_sem, paw_sem, pas_sem,
):
    weeks, rank, columns = jac_ref.shape
    blocks, rhs, width = zfull.shape
    nb = blocks // nw
    kb = columns // width
    wpg = weeks // ns
    mw = lax.axis_index("week")
    ms = lax.axis_index("seg")

    barrier = pltpu.get_barrier_semaphore()
    for i in range(1, nw):
        pl.semaphore_signal(
            barrier, inc=1, device_id={"week": lax.rem(mw + i, nw)}, device_id_type=MESH
        )
    for i in range(1, ns):
        pl.semaphore_signal(
            barrier, inc=1, device_id={"seg": lax.rem(ms + i, ns)}, device_id_type=MESH
        )

    for b in range(nb):
        r_s[b] = right_ref[:, b * width:(b + 1) * width]
    for ref in (x_s, p_s, dp_s, proj, pad, rz_old):
        ref[...] = jnp.zeros_like(ref)
    spread[0] = jnp.zeros((rhs, width), jnp.float32)
    pl.semaphore_wait(barrier, nw + ns - 2)

    def send(src, dst, sems, i, axis, target):
        copy = pltpu.make_async_remote_copy(
            src_ref=src, dst_ref=dst, send_sem=sems.at[0, i - 1], recv_sem=sems.at[1, i - 1],
            device_id={axis: target}, device_id_type=MESH,
        )
        copy.start()
        return copy

    def spread_row(buf, sems, axis, count, me, row):
        buf[me] = row
        return [
            send(buf.at[me], buf.at[me], sems, i, axis, lax.rem(me + i, count))
            for i in range(1, count)
        ]

    def finish(copies):
        for copy in copies:
            copy.wait()

    def to_row(value):
        pad[0:rhs, :] = value
        return jnp.sum(jnp.transpose(pad[...]), axis=0, keepdims=True)

    def from_row(row):
        return jnp.transpose(jnp.broadcast_to(row, (LANES, LANES)))[0:rhs, :]

    def iteration(t, carry):
        def precondition(b, total):
            res = r_s[b]
            z = dot32(res, mtab_ref[kind_ref[b]])
            z_s[b] = z
            zfull[mw * nb + b] = z.astype(jnp.bfloat16)
            return total + res * z

        rz_part = lax.fori_loop(0, nb, precondition, jnp.zeros((rhs, width), jnp.float32))
        rzw_copies = spread_row(rzw, rzw_sem, "week", nw, mw, to_row(rz_part))
        mine = zfull.at[pl.ds(mw * nb, nb)]
        ag_copies = [
            send(mine, mine, ag_sem, i, "week", lax.rem(mw + i, nw)) for i in range(1, nw)
        ]

        def diagonal(b, c):
            dz_s[b] = dot32(z_s[b], dtab_ref[kind_ref[b]])
            return c

        lax.fori_loop(0, nb, diagonal, 0)
        finish(rzw_copies)
        rzs_copies = spread_row(
            rzs, rzs_sem, "seg", ns, ms, jnp.sum(rzw[...], axis=0)
        )
        finish(ag_copies)

        def project(w):
            picked = jnp.concatenate([zfull[wb_ref[w * kb + k]] for k in range(kb)], axis=1)
            return lax.dot_general(
                picked, jac_ref[w], (((1,), (1,)), ((), ())), preferred_element_type=jnp.float32
            )

        sg_copies = []
        for i in range(1, ns):
            group = lax.rem(ms + i, ns)

            def remote_group(j, c):
                w = group * wpg + j
                part[w] = project(w).astype(jnp.bfloat16)
                return c

            lax.fori_loop(0, wpg, remote_group, 0)
            sg_copies.append(
                send(part.at[pl.ds(group * wpg, wpg)], segr.at[i - 1], sg_sem, i, "seg", group)
            )

        def own_group(j, c):
            ownp[j] = project(ms * wpg + j)
            return c

        lax.fori_loop(0, wpg, own_group, 0)
        finish(rzs_copies)
        rz_row = jnp.sum(rzs[...], axis=0)
        ratio = jnp.where(t > 0, rz_row / rz_old[...], jnp.zeros_like(rz_row))
        rz_old[...] = rz_row
        beta = from_row(ratio)
        beta_wide = jnp.concatenate([beta] * (rank // LANES), axis=1)
        finish(sg_copies)
        total = jnp.zeros((rhs, width), jnp.float32)
        for j in range(wpg):
            value = ownp[j]
            for i in range(ns - 1):
                value = value + segr[i, j].astype(jnp.float32)
            value = value + beta_wide * proj[j]
            proj[j] = value
            rounded = value.astype(jnp.bfloat16)
            pbuf[ms * wpg + j] = rounded
            product = value * rounded.astype(jnp.float32)
            for c in range(rank // LANES):
                total = total + product[:, c * LANES:(c + 1) * LANES]
        mine_p = pbuf.at[pl.ds(ms * wpg, wpg)]
        pb_copies = [
            send(mine_p, mine_p, pb_sem, i, "seg", lax.rem(ms + i, ns)) for i in range(1, ns)
        ]

        def directions(b, acc):
            p = z_s[b] + beta * p_s[b]
            dp = dz_s[b] + beta * dp_s[b]
            p_s[b] = p
            dp_s[b] = dp
            return acc + p * dp

        total = lax.fori_loop(0, nb, directions, total)
        pas_copies = spread_row(pas, pas_sem, "seg", ns, ms, to_row(total))

        def back(w):
            values = jnp.dot(pbuf[w], jac_ref[w], preferred_element_type=jnp.float32)
            for k in range(kb):
                spread[1 + w * kb + k] = values[:, k * width:(k + 1) * width]

        def back_group(group):
            def body(j, c):
                back(group * wpg + j)
                return c

            lax.fori_loop(0, wpg, body, 0)

        back_group(ms)
        finish(pas_copies)
        paw_copies = spread_row(
            paw, paw_sem, "week", nw, mw, jnp.sum(pas[...], axis=0)
        )
        finish(pb_copies)
        for i in range(1, ns):
            back_group(lax.rem(ms + i, ns))

        def gathered(b):
            value = spread[inv_ref[b * weeks]]
            for w in range(1, weeks):
                value = value + spread[inv_ref[b * weeks + w]]
            return value

        rs_copies = []
        for i in range(1, nw):
            target = lax.rem(mw + i, nw)

            def remote_block(b, c):
                tbuf[i - 1, b] = gathered(target * nb + b).astype(jnp.bfloat16)
                return c

            lax.fori_loop(0, nb, remote_block, 0)
            rs_copies.append(send(tbuf.at[i - 1], rsr.at[i - 1], rs_sem, i, "week", target))

        def own_block(b, c):
            own[b] = gathered(mw * nb + b) + dp_s[b]
            return c

        lax.fori_loop(0, nb, own_block, 0)
        finish(paw_copies)
        alpha = from_row(rz_row / jnp.sum(paw[...], axis=0))
        finish(rs_copies)

        def update(b, c):
            image = own[b]
            for i in range(nw - 1):
                image = image + rsr[i, b].astype(jnp.float32)
            x_s[b] = x_s[b] + alpha * p_s[b]
            r_s[b] = r_s[b] - alpha * image
            return c

        lax.fori_loop(0, nb, update, 0)
        return carry

    lax.fori_loop(0, ITERS, iteration, 0)
    for b in range(nb):
        x_out[:, b * width:(b + 1) * width] = x_s[b]
        r_out[:, b * width:(b + 1) * width] = r_s[b]


def per_device(nw, ns, right_side, jacobians, week_blocks, block_kind, diagonal_table, precond_table):
    rhs, _, own_length = right_side.shape
    weeks, rank, columns = jacobians.shape
    kb = week_blocks.shape[1]
    width = columns // kb
    nb = own_length // width
    blocks = nb * nw
    wpg = weeks // ns
    slots = 1 + jnp.arange(weeks * kb, dtype=jnp.int32).reshape(weeks, kb)
    numbers = jnp.arange(blocks, dtype=jnp.int32)
    inverse = jnp.sum(
        jnp.where(week_blocks[None] == numbers[:, None, None], slots[None], 0), axis=2
    ).reshape(-1)
    f32, bf16 = jnp.float32, jnp.bfloat16
    smem = pl.BlockSpec(memory_space=pltpu.SMEM)
    vmem = pl.BlockSpec(memory_space=pltpu.VMEM)
    own_state = pltpu.VMEM((nb, rhs, width), f32)

    def sems(count):
        return pltpu.SemaphoreType.DMA((2, count - 1))

    solution, residual = pl.pallas_call(
        functools.partial(kernel, nw, ns),
        out_shape=[jax.ShapeDtypeStruct((rhs, own_length), f32)] * 2,
        in_specs=[smem] * 3 + [vmem] * 4,
        out_specs=[vmem] * 2,
        scratch_shapes=[
            pltpu.VMEM((blocks, rhs, width), bf16),
            pltpu.VMEM((weeks, rhs, rank), bf16),
            pltpu.VMEM((ns - 1, wpg, rhs, rank), bf16),
            pltpu.VMEM((wpg, rhs, rank), f32),
            pltpu.VMEM((wpg, rhs, rank), f32),
            pltpu.VMEM((weeks, rhs, rank), bf16),
            pltpu.VMEM((1 + weeks * kb, rhs, width), f32),
            pltpu.VMEM((nw - 1, nb, rhs, width), bf16),
            pltpu.VMEM((nw - 1, nb, rhs, width), bf16),
            own_state, own_state, own_state, own_state, own_state, own_state, own_state,
            pltpu.VMEM((LANES, LANES), f32),
            pltpu.VMEM((1, LANES), f32),
            pltpu.VMEM((nw, 1, LANES), f32),
            pltpu.VMEM((ns, 1, LANES), f32),
            pltpu.VMEM((nw, 1, LANES), f32),
            pltpu.VMEM((ns, 1, LANES), f32),
            sems(nw), sems(ns), sems(ns), sems(nw), sems(nw), sems(ns), sems(nw), sems(ns),
        ],
        compiler_params=pltpu.CompilerParams(
            collective_id=0, has_side_effects=True, vmem_limit_bytes=48 * 1024 * 1024
        ),
    )(
        week_blocks.reshape(-1), inverse, block_kind.reshape(-1), right_side[:, 0, :],
        jacobians, diagonal_table, precond_table,
    )
    return (solution[:, None, :], residual[:, None, :])


def solution(mesh):
    placed = (
        P(None, "seg", "week"),
        P("week", None, "seg"),
        P("week", "seg"),
        P("seg", "week"),
        P(),
        P(),
    )
    return jax.shard_map(
        functools.partial(per_device, mesh.shape["week"], mesh.shape["seg"]),
        mesh=mesh,
        in_specs=placed,
        out_specs=(P(None, "seg", "week"), P(None, "seg", "week")),
        check_vma=False,
    )
```

```python
import functools

import jax
import jax.numpy as jnp
from jax import lax
from jax.experimental import pallas as pl
from jax.experimental.pallas import tpu as pltpu
from jax.sharding import PartitionSpec as P

ITERS = 4
LANES = 128
CHUNKS = 2
MESH = pl.DeviceIdType.MESH
HIGHEST = lax.Precision.HIGHEST


def dot32(left, right):
    return jnp.dot(left, right, precision=HIGHEST, preferred_element_type=jnp.float32)


def kernel(
    nw, ns, rows, chunks, wb_ref, inv_ref, kind_ref, right_ref, jac_ref, dtab_ref, mtab_ref, x_out, r_out,
    zfull, part, segr, ownp, proj, pbuf, spread, tbuf, rsr, hop, hopr, own, x_s, r_s, z_s, p_s, dz_s, dp_s,
    pad, rz_old, rzw, rzs, paw, pas,
    agz_sem, agy_sem, sg_sem, pb_sem, rsz_sem, rsy_sem, rzw_sem, rzs_sem, paw_sem, pas_sem,
):
    weeks, rank, columns = jac_ref.shape
    blocks, rhs, width = zfull.shape
    nb = blocks // nw
    kb = columns // width
    wpg = weeks // ns
    mw = lax.axis_index("week")
    ms = lax.axis_index("seg")
    lines = nw // rows
    cb = nb // chunks
    line, row = mw // rows, lax.rem(mw, rows)
    ahead = lax.rem(line + 1, lines) * rows + row
    beside = [line * rows + lax.rem(row + j, rows) for j in range(1, rows)]

    def week_at(back):
        return lax.rem(line + lines - back, lines) * rows + row

    barrier = pltpu.get_barrier_semaphore()
    for i in range(1, nw):
        pl.semaphore_signal(
            barrier, inc=1, device_id={"week": lax.rem(mw + i, nw)}, device_id_type=MESH
        )
    for i in range(1, ns):
        pl.semaphore_signal(
            barrier, inc=1, device_id={"seg": lax.rem(ms + i, ns)}, device_id_type=MESH
        )

    for b in range(nb):
        r_s[b] = right_ref[:, b * width:(b + 1) * width]
    for ref in (x_s, p_s, dp_s, proj, pad, rz_old):
        ref[...] = jnp.zeros_like(ref)
    spread[0] = jnp.zeros((rhs, width), jnp.float32)
    pl.semaphore_wait(barrier, nw + ns - 2)

    def send(src, dst, sems, i, axis, target):
        copy = pltpu.make_async_remote_copy(
            src_ref=src, dst_ref=dst, send_sem=sems.at[0, i - 1], recv_sem=sems.at[1, i - 1],
            device_id={axis: target}, device_id_type=MESH,
        )
        copy.start()
        return copy

    def spread_row(buf, sems, axis, count, me, row):
        buf[me] = row
        return [
            send(buf.at[me], buf.at[me], sems, i, axis, lax.rem(me + i, count))
            for i in range(1, count)
        ]

    def finish(copies):
        for copy in copies:
            copy.wait()

    def to_row(value):
        pad[0:rhs, :] = value
        return jnp.sum(jnp.transpose(pad[...]), axis=0, keepdims=True)

    def from_row(row):
        return jnp.transpose(jnp.broadcast_to(row, (LANES, LANES)))[0:rhs, :]

    def iteration(t, carry):
        def precondition(b, total):
            res = r_s[b]
            z = dot32(res, mtab_ref[kind_ref[b]])
            z_s[b] = z
            zfull[mw * nb + b] = z.astype(jnp.bfloat16)
            return total + res * z

        rz_part = lax.fori_loop(0, nb, precondition, jnp.zeros((rhs, width), jnp.float32))
        rzw_copies = spread_row(rzw, rzw_sem, "week", nw, mw, to_row(rz_part))
        ring, across = [], []

        def pass_on(s, c):
            piece = zfull.at[pl.ds(week_at(s) * nb + c * cb, cb)]
            if s < lines - 1:
                ring.append(send(piece, piece, agz_sem, s * chunks + c + 1, "week", ahead))
            for j in range(rows - 1):
                place = (j * lines + s) * chunks + c + 1
                across.append(send(piece, piece, agy_sem, place, "week", beside[j]))

        for c in range(chunks):
            pass_on(0, c)

        def diagonal(b, c):
            dz_s[b] = dot32(z_s[b], dtab_ref[kind_ref[b]])
            return c

        lax.fori_loop(0, nb, diagonal, 0)
        finish(rzw_copies)
        rzs_copies = spread_row(
            rzs, rzs_sem, "seg", ns, ms, jnp.sum(rzw[...], axis=0)
        )
        for s in range(1, lines):
            for c in range(chunks):
                ring[(s - 1) * chunks + c].wait_recv()
                pass_on(s, c)
        for copy in ring:
            copy.wait_send()
        finish(across)

        def project(w):
            picked = jnp.concatenate([zfull[wb_ref[w * kb + k]] for k in range(kb)], axis=1)
            return lax.dot_general(
                picked, jac_ref[w], (((1,), (1,)), ((), ())), preferred_element_type=jnp.float32
            )

        sg_copies = []
        for i in range(1, ns):
            group = lax.rem(ms + i, ns)

            def remote_group(j, c):
                w = group * wpg + j
                part[w] = project(w).astype(jnp.bfloat16)
                return c

            lax.fori_loop(0, wpg, remote_group, 0)
            sg_copies.append(
                send(part.at[pl.ds(group * wpg, wpg)], segr.at[i - 1], sg_sem, i, "seg", group)
            )

        def own_group(j, c):
            ownp[j] = project(ms * wpg + j)
            return c

        lax.fori_loop(0, wpg, own_group, 0)
        finish(rzs_copies)
        rz_row = jnp.sum(rzs[...], axis=0)
        ratio = jnp.where(t > 0, rz_row / rz_old[...], jnp.zeros_like(rz_row))
        rz_old[...] = rz_row
        beta = from_row(ratio)
        beta_wide = jnp.concatenate([beta] * (rank // LANES), axis=1)
        finish(sg_copies)
        total = jnp.zeros((rhs, width), jnp.float32)
        for j in range(wpg):
            value = ownp[j]
            for i in range(ns - 1):
                value = value + segr[i, j].astype(jnp.float32)
            value = value + beta_wide * proj[j]
            proj[j] = value
            rounded = value.astype(jnp.bfloat16)
            pbuf[ms * wpg + j] = rounded
            product = value * rounded.astype(jnp.float32)
            for c in range(rank // LANES):
                total = total + product[:, c * LANES:(c + 1) * LANES]
        mine_p = pbuf.at[pl.ds(ms * wpg, wpg)]
        pb_copies = [
            send(mine_p, mine_p, pb_sem, i, "seg", lax.rem(ms + i, ns)) for i in range(1, ns)
        ]

        def directions(b, acc):
            p = z_s[b] + beta * p_s[b]
            dp = dz_s[b] + beta * dp_s[b]
            p_s[b] = p
            dp_s[b] = dp
            return acc + p * dp

        total = lax.fori_loop(0, nb, directions, total)
        pas_copies = spread_row(pas, pas_sem, "seg", ns, ms, to_row(total))

        def back(w):
            values = jnp.dot(pbuf[w], jac_ref[w], preferred_element_type=jnp.float32)
            for k in range(kb):
                spread[1 + w * kb + k] = values[:, k * width:(k + 1) * width]

        def back_group(group):
            def body(j, c):
                back(group * wpg + j)
                return c

            lax.fori_loop(0, wpg, body, 0)

        back_group(ms)
        finish(pas_copies)
        paw_copies = spread_row(
            paw, paw_sem, "week", nw, mw, jnp.sum(pas[...], axis=0)
        )
        finish(pb_copies)
        for i in range(1, ns):
            back_group(lax.rem(ms + i, ns))

        def gathered(b):
            value = spread[inv_ref[b * weeks]]
            for w in range(1, weeks):
                value = value + spread[inv_ref[b * weeks + w]]
            return value

        aside = {}
        for s in range(lines):
            for c in range(chunks):
                for j in range(rows - 1):
                    target = lax.rem(line + 2 * lines - 1 - s, lines) * rows + lax.rem(
                        row + j + 1, rows
                    )

                    def beside_block(b, carry):
                        tbuf[j, s, c * cb + b] = gathered(
                            target * nb + c * cb + b
                        ).astype(jnp.bfloat16)
                        return carry

                    lax.fori_loop(0, cb, beside_block, 0)
                    piece = pl.ds(c * cb, cb)
                    aside[j, s, c] = send(
                        tbuf.at[j, s, piece], rsr.at[j, s, piece], rsy_sem,
                        (j * lines + s) * chunks + c + 1, "week", beside[j],
                    )
        hops = {}
        for s in range(lines - 1):
            for c in range(chunks):
                target = lax.rem(line + 2 * lines - 1 - s, lines) * rows + row
                for j in range(rows - 1):
                    aside[j, s, c].wait_recv()
                if s > 0:
                    hops[s - 1, c].wait_recv()

                def hop_block(b, carry):
                    place = c * cb + b
                    value = gathered(target * nb + place)
                    for j in range(rows - 1):
                        value = value + rsr[j, s, place].astype(jnp.float32)
                    if s > 0:
                        value = value + hopr[s - 1, place].astype(jnp.float32)
                    hop[s, place] = value.astype(jnp.bfloat16)
                    return carry

                lax.fori_loop(0, cb, hop_block, 0)
                piece = pl.ds(c * cb, cb)
                hops[s, c] = send(
                    hop.at[s, piece], hopr.at[s, piece], rsz_sem, s * chunks + c + 1, "week", ahead
                )

        def own_block(b, c):
            own[b] = gathered(mw * nb + b) + dp_s[b]
            return c

        lax.fori_loop(0, nb, own_block, 0)
        finish(paw_copies)
        alpha = from_row(rz_row / jnp.sum(paw[...], axis=0))
        for c in range(chunks):
            for j in range(rows - 1):
                aside[j, lines - 1, c].wait_recv()
            hops[lines - 2, c].wait_recv()
        for copy in list(aside.values()) + list(hops.values()):
            copy.wait_send()

        def update(b, c):
            image = own[b] + hopr[lines - 2, b].astype(jnp.float32)
            for j in range(rows - 1):
                image = image + rsr[j, lines - 1, b].astype(jnp.float32)
            x_s[b] = x_s[b] + alpha * p_s[b]
            r_s[b] = r_s[b] - alpha * image
            return c

        lax.fori_loop(0, nb, update, 0)
        return carry

    lax.fori_loop(0, ITERS, iteration, 0)
    for b in range(nb):
        x_out[:, b * width:(b + 1) * width] = x_s[b]
        r_out[:, b * width:(b + 1) * width] = r_s[b]


def per_device(nw, ns, right_side, jacobians, week_blocks, block_kind, diagonal_table, precond_table):
    rhs, _, own_length = right_side.shape
    weeks, rank, columns = jacobians.shape
    kb = week_blocks.shape[1]
    width = columns // kb
    nb = own_length // width
    blocks = nb * nw
    wpg = weeks // ns
    rows = 1
    while 4 * rows * rows <= nw:
        rows *= 2
    lines = nw // rows
    chunks = min(CHUNKS, nb)
    slots = 1 + jnp.arange(weeks * kb, dtype=jnp.int32).reshape(weeks, kb)
    numbers = jnp.arange(blocks, dtype=jnp.int32)
    inverse = jnp.sum(
        jnp.where(week_blocks[None] == numbers[:, None, None], slots[None], 0), axis=2
    ).reshape(-1)
    f32, bf16 = jnp.float32, jnp.bfloat16
    smem = pl.BlockSpec(memory_space=pltpu.SMEM)
    vmem = pl.BlockSpec(memory_space=pltpu.VMEM)
    own_state = pltpu.VMEM((nb, rhs, width), f32)

    def sems(count):
        return pltpu.SemaphoreType.DMA((2, count - 1))

    solution, residual = pl.pallas_call(
        functools.partial(kernel, nw, ns, rows, chunks),
        out_shape=[jax.ShapeDtypeStruct((rhs, own_length), f32)] * 2,
        in_specs=[smem] * 3 + [vmem] * 4,
        out_specs=[vmem] * 2,
        scratch_shapes=[
            pltpu.VMEM((blocks, rhs, width), bf16),
            pltpu.VMEM((weeks, rhs, rank), bf16),
            pltpu.VMEM((ns - 1, wpg, rhs, rank), bf16),
            pltpu.VMEM((wpg, rhs, rank), f32),
            pltpu.VMEM((wpg, rhs, rank), f32),
            pltpu.VMEM((weeks, rhs, rank), bf16),
            pltpu.VMEM((1 + weeks * kb, rhs, width), f32),
            pltpu.VMEM((rows - 1, lines, nb, rhs, width), bf16),
            pltpu.VMEM((rows - 1, lines, nb, rhs, width), bf16),
            pltpu.VMEM((lines - 1, nb, rhs, width), bf16),
            pltpu.VMEM((lines - 1, nb, rhs, width), bf16),
            own_state, own_state, own_state, own_state, own_state, own_state, own_state,
            pltpu.VMEM((LANES, LANES), f32),
            pltpu.VMEM((1, LANES), f32),
            pltpu.VMEM((nw, 1, LANES), f32),
            pltpu.VMEM((ns, 1, LANES), f32),
            pltpu.VMEM((nw, 1, LANES), f32),
            pltpu.VMEM((ns, 1, LANES), f32),
            sems((lines - 1) * chunks + 1), sems((rows - 1) * lines * chunks + 1),
            sems(ns), sems(ns),
            sems((lines - 1) * chunks + 1), sems((rows - 1) * lines * chunks + 1),
            sems(nw), sems(ns), sems(nw), sems(ns),
        ],
        compiler_params=pltpu.CompilerParams(
            collective_id=0, has_side_effects=True, vmem_limit_bytes=48 * 1024 * 1024
        ),
    )(
        week_blocks.reshape(-1), inverse, block_kind.reshape(-1), right_side[:, 0, :],
        jacobians, diagonal_table, precond_table,
    )
    return (solution[:, None, :], residual[:, None, :])


def solution(mesh):
    placed = (
        P(None, "seg", "week"),
        P("week", None, "seg"),
        P("week", "seg"),
        P("seg", "week"),
        P(),
        P(),
    )
    return jax.shard_map(
        functools.partial(per_device, mesh.shape["week"], mesh.shape["seg"]),
        mesh=mesh,
        in_specs=placed,
        out_specs=(P(None, "seg", "week"), P(None, "seg", "week")),
        check_vma=False,
    )
```

```python
import functools

import jax
import jax.numpy as jnp
from jax import lax
from jax.experimental import pallas as pl
from jax.experimental.pallas import tpu as pltpu
from jax.sharding import PartitionSpec as P

ITERS = 4
LANES = 128
CHUNKS = 4
MESH = pl.DeviceIdType.MESH
HIGHEST = lax.Precision.HIGHEST


def dot32(left, right):
    return jnp.dot(left, right, precision=HIGHEST, preferred_element_type=jnp.float32)


def kernel(
    nw, ns, rows, chunks, wb_ref, inv_ref, kind_ref, right_ref, jac_hbm, dtab_ref, mtab_ref, x_out, r_out,
    jac_ref, jac_sem,    zfull, part, segr, ownp, proj, pbuf, spread, tbuf, rsr, hop, hopr, own, x_s, r_s, z_s, p_s, dz_s, dp_s,
    pad, rz_old, rzw, rzs, paw, pas,
    agz_sem, agy_sem, sg_sem, pb_sem, rsz_sem, rsy_sem, rzw_sem, rzs_sem, paw_sem, pas_sem,
):
    weeks, rank, columns = jac_ref.shape
    blocks, rhs, width = zfull.shape
    load = pltpu.make_async_copy(jac_hbm, jac_ref, jac_sem)
    load.start()
    nb = blocks // nw
    kb = columns // width
    wpg = weeks // ns
    mw = lax.axis_index("week")
    ms = lax.axis_index("seg")
    lines = nw // rows
    cb = nb // chunks
    line, row = mw // rows, lax.rem(mw, rows)
    ahead = lax.rem(line + 1, lines) * rows + row
    beside = [line * rows + lax.rem(row + j, rows) for j in range(1, rows)]

    def week_at(back):
        return lax.rem(line + lines - back, lines) * rows + row

    barrier = pltpu.get_barrier_semaphore()
    for i in range(1, nw):
        pl.semaphore_signal(
            barrier, inc=1, device_id={"week": lax.rem(mw + i, nw)}, device_id_type=MESH
        )
    for i in range(1, ns):
        pl.semaphore_signal(
            barrier, inc=1, device_id={"seg": lax.rem(ms + i, ns)}, device_id_type=MESH
        )

    for b in range(nb):
        r_s[b] = right_ref[:, b * width:(b + 1) * width]
    for ref in (x_s, p_s, dp_s, proj, pad, rz_old):
        ref[...] = jnp.zeros_like(ref)
    spread[0] = jnp.zeros((rhs, width), jnp.float32)
    pl.semaphore_wait(barrier, nw + ns - 2)

    def send(src, dst, sems, i, axis, target):
        copy = pltpu.make_async_remote_copy(
            src_ref=src, dst_ref=dst, send_sem=sems.at[0, i - 1], recv_sem=sems.at[1, i - 1],
            device_id={axis: target}, device_id_type=MESH,
        )
        copy.start()
        return copy

    def spread_row(buf, sems, axis, count, me, row):
        buf[me] = row
        return [
            send(buf.at[me], buf.at[me], sems, i, axis, lax.rem(me + i, count))
            for i in range(1, count)
        ]

    def finish(copies):
        for copy in copies:
            copy.wait()

    def to_row(value):
        pad[0:rhs, :] = value
        return jnp.sum(jnp.transpose(pad[...]), axis=0, keepdims=True)

    def from_row(row):
        return jnp.transpose(jnp.broadcast_to(row, (LANES, LANES)))[0:rhs, :]

    def iteration(t, carry):
        def precondition(b, total):
            res = r_s[b]
            z = dot32(res, mtab_ref[kind_ref[b]])
            z_s[b] = z
            zfull[mw * nb + b] = z.astype(jnp.bfloat16)
            return total + res * z

        ring, across = [], []

        def pass_on(s, c):
            piece = zfull.at[pl.ds(week_at(s) * nb + c * cb, cb)]
            if s < lines - 1:
                ring.append(send(piece, piece, agz_sem, s * chunks + c + 1, "week", ahead))
            for j in range(rows - 1):
                place = (j * lines + s) * chunks + c + 1
                across.append(send(piece, piece, agy_sem, place, "week", beside[j]))

        rz_part = jnp.zeros((rhs, width), jnp.float32)
        for c in range(chunks):
            rz_part = lax.fori_loop(c * cb, (c + 1) * cb, precondition, rz_part)
            pass_on(0, c)
        rzw_copies = spread_row(rzw, rzw_sem, "week", nw, mw, to_row(rz_part))

        def diagonal(b, c):
            dz_s[b] = dot32(z_s[b], dtab_ref[kind_ref[b]])
            return c

        lax.fori_loop(0, nb, diagonal, 0)
        for s in range(1, lines):
            for c in range(chunks):
                ring[(s - 1) * chunks + c].wait_recv()
                pass_on(s, c)
        for copy in ring:
            copy.wait_send()
        finish(across)
        finish(rzw_copies)
        rzs_copies = spread_row(
            rzs, rzs_sem, "seg", ns, ms, jnp.sum(rzw[...], axis=0)
        )

        @pl.when(t == 0)
        def _():
            load.wait()

        def project(w):
            picked = jnp.concatenate([zfull[wb_ref[w * kb + k]] for k in range(kb)], axis=1)
            return lax.dot_general(
                picked, jac_ref[w], (((1,), (1,)), ((), ())), preferred_element_type=jnp.float32
            )

        sg_copies = []
        order = sorted(range(1, ns), key=lambda i: abs(i - ns // 2))
        for i in order:
            group = lax.rem(ms + i, ns)

            def remote_group(j, c):
                w = group * wpg + j
                part[w] = project(w).astype(jnp.bfloat16)
                return c

            lax.fori_loop(0, wpg, remote_group, 0)
            sg_copies.append(
                send(part.at[pl.ds(group * wpg, wpg)], segr.at[i - 1], sg_sem, i, "seg", group)
            )

        def own_group(j, c):
            ownp[j] = project(ms * wpg + j)
            return c

        lax.fori_loop(0, wpg, own_group, 0)
        finish(rzs_copies)
        rz_row = jnp.sum(rzs[...], axis=0)
        ratio = jnp.where(t > 0, rz_row / rz_old[...], jnp.zeros_like(rz_row))
        rz_old[...] = rz_row
        beta = from_row(ratio)
        beta_wide = jnp.concatenate([beta] * (rank // LANES), axis=1)
        finish(sg_copies)
        total = jnp.zeros((rhs, width), jnp.float32)
        for j in range(wpg):
            value = ownp[j]
            for i in range(ns - 1):
                value = value + segr[i, j].astype(jnp.float32)
            value = value + beta_wide * proj[j]
            proj[j] = value
            rounded = value.astype(jnp.bfloat16)
            pbuf[ms * wpg + j] = rounded
            product = value * rounded.astype(jnp.float32)
            for c in range(rank // LANES):
                total = total + product[:, c * LANES:(c + 1) * LANES]
        mine_p = pbuf.at[pl.ds(ms * wpg, wpg)]
        pb_copies = [
            send(mine_p, mine_p, pb_sem, i, "seg", lax.rem(ms + i, ns)) for i in range(1, ns)
        ]

        def directions(b, acc):
            p = z_s[b] + beta * p_s[b]
            dp = dz_s[b] + beta * dp_s[b]
            p_s[b] = p
            dp_s[b] = dp
            return acc + p * dp

        total = lax.fori_loop(0, nb, directions, total)
        pas_copies = spread_row(pas, pas_sem, "seg", ns, ms, to_row(total))

        def back(w):
            values = jnp.dot(pbuf[w], jac_ref[w], preferred_element_type=jnp.float32)
            for k in range(kb):
                spread[1 + w * kb + k] = values[:, k * width:(k + 1) * width]

        def back_group(group):
            def body(j, c):
                back(group * wpg + j)
                return c

            lax.fori_loop(0, wpg, body, 0)

        back_group(ms)
        finish(pas_copies)
        paw_copies = spread_row(
            paw, paw_sem, "week", nw, mw, jnp.sum(pas[...], axis=0)
        )
        finish(pb_copies)
        for i in range(1, ns):
            back_group(lax.rem(ms + i, ns))

        def gathered(b):
            value = spread[inv_ref[b * weeks]]
            for w in range(1, weeks):
                value = value + spread[inv_ref[b * weeks + w]]
            return value

        aside = {}
        for s in range(lines):
            for c in range(chunks):
                for j in range(rows - 1):
                    target = lax.rem(line + 2 * lines - 1 - s, lines) * rows + lax.rem(
                        row + j + 1, rows
                    )

                    def beside_block(b, carry):
                        tbuf[j, s, c * cb + b] = gathered(
                            target * nb + c * cb + b
                        ).astype(jnp.bfloat16)
                        return carry

                    lax.fori_loop(0, cb, beside_block, 0)
                    piece = pl.ds(c * cb, cb)
                    aside[j, s, c] = send(
                        tbuf.at[j, s, piece], rsr.at[j, s, piece], rsy_sem,
                        (j * lines + s) * chunks + c + 1, "week", beside[j],
                    )
        hops = {}
        for s in range(lines - 1):
            for c in range(chunks):
                target = lax.rem(line + 2 * lines - 1 - s, lines) * rows + row
                for j in range(rows - 1):
                    aside[j, s, c].wait_recv()
                if s > 0:
                    hops[s - 1, c].wait_recv()

                def hop_block(b, carry):
                    place = c * cb + b
                    value = gathered(target * nb + place)
                    for j in range(rows - 1):
                        value = value + rsr[j, s, place].astype(jnp.float32)
                    if s > 0:
                        value = value + hopr[s - 1, place].astype(jnp.float32)
                    hop[s, place] = value.astype(jnp.bfloat16)
                    return carry

                lax.fori_loop(0, cb, hop_block, 0)
                piece = pl.ds(c * cb, cb)
                hops[s, c] = send(
                    hop.at[s, piece], hopr.at[s, piece], rsz_sem, s * chunks + c + 1, "week", ahead
                )

        def own_block(b, c):
            own[b] = gathered(mw * nb + b) + dp_s[b]
            return c

        lax.fori_loop(0, nb, own_block, 0)
        finish(paw_copies)
        alpha = from_row(rz_row / jnp.sum(paw[...], axis=0))

        def advance(b, c):
            x_s[b] = x_s[b] + alpha * p_s[b]
            return c

        lax.fori_loop(0, nb, advance, 0)
        def update(b, c):
            image = own[b] + hopr[lines - 2, b].astype(jnp.float32)
            for j in range(rows - 1):
                image = image + rsr[j, lines - 1, b].astype(jnp.float32)
            r_s[b] = r_s[b] - alpha * image
            return c

        for c in range(chunks):
            for j in range(rows - 1):
                aside[j, lines - 1, c].wait_recv()
            hops[lines - 2, c].wait_recv()
            lax.fori_loop(c * cb, (c + 1) * cb, update, 0)
        for copy in list(aside.values()) + list(hops.values()):
            copy.wait_send()
        return carry

    lax.fori_loop(0, ITERS, iteration, 0)
    for b in range(nb):
        x_out[:, b * width:(b + 1) * width] = x_s[b]
        r_out[:, b * width:(b + 1) * width] = r_s[b]


def per_device(nw, ns, right_side, jacobians, week_blocks, block_kind, diagonal_table, precond_table):
    rhs, _, own_length = right_side.shape
    weeks, rank, columns = jacobians.shape
    kb = week_blocks.shape[1]
    width = columns // kb
    nb = own_length // width
    blocks = nb * nw
    wpg = weeks // ns
    rows = 1
    while 4 * rows * rows <= nw:
        rows *= 2
    lines = nw // rows
    chunks = min(CHUNKS, nb)
    slots = 1 + jnp.arange(weeks * kb, dtype=jnp.int32).reshape(weeks, kb)
    numbers = jnp.arange(blocks, dtype=jnp.int32)
    inverse = jnp.sum(
        jnp.where(week_blocks[None] == numbers[:, None, None], slots[None], 0), axis=2
    ).reshape(-1)
    f32, bf16 = jnp.float32, jnp.bfloat16
    smem = pl.BlockSpec(memory_space=pltpu.SMEM)
    vmem = pl.BlockSpec(memory_space=pltpu.VMEM)
    own_state = pltpu.VMEM((nb, rhs, width), f32)

    def sems(count):
        return pltpu.SemaphoreType.DMA((2, count - 1))

    solution, residual = pl.pallas_call(
        functools.partial(kernel, nw, ns, rows, chunks),
        out_shape=[jax.ShapeDtypeStruct((rhs, own_length), f32)] * 2,
        in_specs=[smem] * 3 + [vmem, pl.BlockSpec(memory_space=pl.ANY), vmem, vmem],
        out_specs=[vmem] * 2,
        scratch_shapes=[
            pltpu.VMEM(jacobians.shape, jacobians.dtype),
            pltpu.SemaphoreType.DMA,
            pltpu.VMEM((blocks, rhs, width), bf16),
            pltpu.VMEM((weeks, rhs, rank), bf16),
            pltpu.VMEM((ns - 1, wpg, rhs, rank), bf16),
            pltpu.VMEM((wpg, rhs, rank), f32),
            pltpu.VMEM((wpg, rhs, rank), f32),
            pltpu.VMEM((weeks, rhs, rank), bf16),
            pltpu.VMEM((1 + weeks * kb, rhs, width), f32),
            pltpu.VMEM((rows - 1, lines, nb, rhs, width), bf16),
            pltpu.VMEM((rows - 1, lines, nb, rhs, width), bf16),
            pltpu.VMEM((lines - 1, nb, rhs, width), bf16),
            pltpu.VMEM((lines - 1, nb, rhs, width), bf16),
            own_state, own_state, own_state, own_state, own_state, own_state, own_state,
            pltpu.VMEM((LANES, LANES), f32),
            pltpu.VMEM((1, LANES), f32),
            pltpu.VMEM((nw, 1, LANES), f32),
            pltpu.VMEM((ns, 1, LANES), f32),
            pltpu.VMEM((nw, 1, LANES), f32),
            pltpu.VMEM((ns, 1, LANES), f32),
            sems((lines - 1) * chunks + 1), sems((rows - 1) * lines * chunks + 1),
            sems(ns), sems(ns),
            sems((lines - 1) * chunks + 1), sems((rows - 1) * lines * chunks + 1),
            sems(nw), sems(ns), sems(nw), sems(ns),
        ],
        compiler_params=pltpu.CompilerParams(
            collective_id=0, has_side_effects=True, vmem_limit_bytes=48 * 1024 * 1024
        ),
    )(
        week_blocks.reshape(-1), inverse, block_kind.reshape(-1), right_side[:, 0, :],
        jacobians, diagonal_table, precond_table,
    )
    return (solution[:, None, :], residual[:, None, :])


def solution(mesh):
    placed = (
        P(None, "seg", "week"),
        P("week", None, "seg"),
        P("week", "seg"),
        P("seg", "week"),
        P(),
        P(),
    )
    return jax.shard_map(
        functools.partial(per_device, mesh.shape["week"], mesh.shape["seg"]),
        mesh=mesh,
        in_specs=placed,
        out_specs=(P(None, "seg", "week"), P(None, "seg", "week")),
        check_vma=False,
    )
```

```python
import functools

import jax
import jax.numpy as jnp
from jax import lax
from jax.experimental import pallas as pl
from jax.experimental.pallas import tpu as pltpu
from jax.sharding import PartitionSpec as P

ITERS = 4
LANES = 128
CHUNKS = 8
MESH = pl.DeviceIdType.MESH
HIGHEST = lax.Precision.HIGHEST


def dot32(left, right):
    return jnp.dot(left, right, precision=HIGHEST, preferred_element_type=jnp.float32)


def kernel(
    nw, ns, rows, chunks, wb_ref, inv_ref, kind_ref, right_ref, jac_hbm, dtab_ref, mtab_ref, x_out, r_out,
    jac_ref, jac_sem,    zfull, part, segr, ownp, proj, pbuf, spread, tbuf, rsr, hop, hopr, own, x_s, r_s, z_s, p_s, dz_s, dp_s,
    pad, rz_old, rzw, rzs, paw, pas,
    agz_sem, agy_sem, agx_sem, sg_sem, pb_sem, rsz_sem, rsy_sem, rzw_sem, rzs_sem, paw_sem, pas_sem,
):
    weeks, rank, columns = jac_ref.shape
    blocks, rhs, width = zfull.shape
    load = pltpu.make_async_copy(jac_hbm, jac_ref, jac_sem)
    load.start()
    nb = blocks // nw
    kb = columns // width
    wpg = weeks // ns
    mw = lax.axis_index("week")
    ms = lax.axis_index("seg")
    lines = nw // rows
    cb = nb // chunks
    early = chunks // 8
    line, row = mw // rows, lax.rem(mw, rows)
    ahead = lax.rem(line + 1, lines) * rows + row
    beside = [line * rows + lax.rem(row + j, rows) for j in range(1, rows)]

    def week_at(back):
        return lax.rem(line + lines - back, lines) * rows + row

    barrier = pltpu.get_barrier_semaphore()
    for i in range(1, nw):
        pl.semaphore_signal(
            barrier, inc=1, device_id={"week": lax.rem(mw + i, nw)}, device_id_type=MESH
        )
    for i in range(1, ns):
        pl.semaphore_signal(
            barrier, inc=1, device_id={"seg": lax.rem(ms + i, ns)}, device_id_type=MESH
        )

    for b in range(nb):
        r_s[b] = right_ref[:, b * width:(b + 1) * width]
    for ref in (x_s, p_s, dp_s, proj, pad, rz_old):
        ref[...] = jnp.zeros_like(ref)
    spread[0] = jnp.zeros((rhs, width), jnp.float32)
    pl.semaphore_wait(barrier, nw + ns - 2)

    def send(src, dst, sems, i, axis, target):
        copy = pltpu.make_async_remote_copy(
            src_ref=src, dst_ref=dst, send_sem=sems.at[0, i - 1], recv_sem=sems.at[1, i - 1],
            device_id={axis: target}, device_id_type=MESH,
        )
        copy.start()
        return copy

    def spread_row(buf, sems, axis, count, me, row):
        buf[me] = row
        return [
            send(buf.at[me], buf.at[me], sems, i, axis, lax.rem(me + i, count))
            for i in range(1, count)
        ]

    def finish(copies):
        for copy in copies:
            copy.wait()

    def to_row(value):
        pad[0:rhs, :] = value
        return jnp.sum(jnp.transpose(pad[...]), axis=0, keepdims=True)

    def from_row(row):
        return jnp.transpose(jnp.broadcast_to(row, (LANES, LANES)))[0:rhs, :]

    def iteration(t, carry):
        def precondition(b, total):
            res = r_s[b]
            z = dot32(res, mtab_ref[kind_ref[b]])
            z_s[b] = z
            zfull[mw * nb + b] = z.astype(jnp.bfloat16)
            return total + res * z

        ring, across, relay = [], [], {}

        def pass_on(s, c):
            piece = zfull.at[pl.ds(week_at(s) * nb + c * cb, cb)]
            if s < lines - 1:
                ring.append(send(piece, piece, agz_sem, s * chunks + c + 1, "week", ahead))
            if s > 0 and c < early:
                return
            for j in range(rows - 1):
                place = (j * lines + s) * chunks + c + 1
                copy = send(piece, piece, agy_sem, place, "week", beside[j])
                if c < early:
                    relay[j, 0, c] = copy
                else:
                    across.append(copy)

        rz_part = jnp.zeros((rhs, width), jnp.float32)
        for c in range(chunks):
            rz_part = lax.fori_loop(c * cb, (c + 1) * cb, precondition, rz_part)
            pass_on(0, c)
        rzw_copies = spread_row(rzw, rzw_sem, "week", nw, mw, to_row(rz_part))

        def diagonal(b, c):
            dz_s[b] = dot32(z_s[b], dtab_ref[kind_ref[b]])
            return c

        lax.fori_loop(0, nb, diagonal, 0)
        for s in range(1, lines):
            for c in range(chunks):
                ring[(s - 1) * chunks + c].wait_recv()
                pass_on(s, c)
                if c >= early:
                    continue
                for j in range(rows - 1):
                    relay[j, s - 1, c].wait_recv()
                    origin = lax.rem(line + lines - s + 1, lines) * rows + lax.rem(
                        row + rows - 1 - j, rows
                    )
                    piece = zfull.at[pl.ds(origin * nb + c * cb, cb)]
                    place = (j * (lines - 1) + s - 1) * early + c + 1
                    relay[j, s, c] = send(piece, piece, agx_sem, place, "week", ahead)
        for (j, s, c), copy in relay.items():
            if s == lines - 1:
                copy.wait_recv()
            copy.wait_send()
        for copy in ring:
            copy.wait_send()
        finish(across)
        finish(rzw_copies)
        rzs_copies = spread_row(
            rzs, rzs_sem, "seg", ns, ms, jnp.sum(rzw[...], axis=0)
        )

        @pl.when(t == 0)
        def _():
            load.wait()

        def project(w):
            picked = jnp.concatenate([zfull[wb_ref[w * kb + k]] for k in range(kb)], axis=1)
            return lax.dot_general(
                picked, jac_ref[w], (((1,), (1,)), ((), ())), preferred_element_type=jnp.float32
            )

        sg_copies = []
        order = sorted(range(1, ns), key=lambda i: abs(i - ns // 2))
        for i in order:
            group = lax.rem(ms + i, ns)

            def remote_group(j, c):
                w = group * wpg + j
                part[w] = project(w).astype(jnp.bfloat16)
                return c

            lax.fori_loop(0, wpg, remote_group, 0)
            sg_copies.append(
                send(part.at[pl.ds(group * wpg, wpg)], segr.at[i - 1], sg_sem, i, "seg", group)
            )

        def own_group(j, c):
            ownp[j] = project(ms * wpg + j)
            return c

        lax.fori_loop(0, wpg, own_group, 0)
        finish(rzs_copies)
        rz_row = jnp.sum(rzs[...], axis=0)
        ratio = jnp.where(t > 0, rz_row / rz_old[...], jnp.zeros_like(rz_row))
        rz_old[...] = rz_row
        beta = from_row(ratio)
        beta_wide = jnp.concatenate([beta] * (rank // LANES), axis=1)
        finish(sg_copies)
        total = jnp.zeros((rhs, width), jnp.float32)
        for j in range(wpg):
            value = ownp[j]
            for i in range(ns - 1):
                value = value + segr[i, j].astype(jnp.float32)
            value = value + beta_wide * proj[j]
            proj[j] = value
            rounded = value.astype(jnp.bfloat16)
            pbuf[ms * wpg + j] = rounded
            product = value * rounded.astype(jnp.float32)
            for c in range(rank // LANES):
                total = total + product[:, c * LANES:(c + 1) * LANES]
        mine_p = pbuf.at[pl.ds(ms * wpg, wpg)]
        pb_copies = [
            send(mine_p, mine_p, pb_sem, i, "seg", lax.rem(ms + i, ns)) for i in range(1, ns)
        ]

        def directions(b, acc):
            p = z_s[b] + beta * p_s[b]
            dp = dz_s[b] + beta * dp_s[b]
            p_s[b] = p
            dp_s[b] = dp
            return acc + p * dp

        total = lax.fori_loop(0, nb, directions, total)
        pas_copies = spread_row(pas, pas_sem, "seg", ns, ms, to_row(total))

        def back(w):
            values = jnp.dot(pbuf[w], jac_ref[w], preferred_element_type=jnp.float32)
            for k in range(kb):
                spread[1 + w * kb + k] = values[:, k * width:(k + 1) * width]

        def back_group(group):
            def body(j, c):
                back(group * wpg + j)
                return c

            lax.fori_loop(0, wpg, body, 0)

        back_group(ms)
        finish(pas_copies)
        paw_copies = spread_row(
            paw, paw_sem, "week", nw, mw, jnp.sum(pas[...], axis=0)
        )
        finish(pb_copies)
        for i in range(1, ns):
            back_group(lax.rem(ms + i, ns))

        def gathered(b):
            value = spread[inv_ref[b * weeks]]
            for w in range(1, weeks):
                value = value + spread[inv_ref[b * weeks + w]]
            return value

        aside = {}
        for s in range(lines):
            for c in range(chunks):
                for j in range(rows - 1):
                    target = lax.rem(line + 2 * lines - 1 - s, lines) * rows + lax.rem(
                        row + j + 1, rows
                    )

                    def beside_block(b, carry):
                        tbuf[j, s, c * cb + b] = gathered(
                            target * nb + c * cb + b
                        ).astype(jnp.bfloat16)
                        return carry

                    lax.fori_loop(0, cb, beside_block, 0)
                    piece = pl.ds(c * cb, cb)
                    aside[j, s, c] = send(
                        tbuf.at[j, s, piece], rsr.at[j, s, piece], rsy_sem,
                        (j * lines + s) * chunks + c + 1, "week", beside[j],
                    )
        hops = {}
        for s in range(lines - 1):
            for c in range(chunks):
                target = lax.rem(line + 2 * lines - 1 - s, lines) * rows + row
                for j in range(rows - 1):
                    aside[j, s, c].wait_recv()
                if s > 0:
                    hops[s - 1, c].wait_recv()

                def hop_block(b, carry):
                    place = c * cb + b
                    value = gathered(target * nb + place)
                    for j in range(rows - 1):
                        value = value + rsr[j, s, place].astype(jnp.float32)
                    if s > 0:
                        value = value + hopr[s - 1, place].astype(jnp.float32)
                    hop[s, place] = value.astype(jnp.bfloat16)
                    return carry

                lax.fori_loop(0, cb, hop_block, 0)
                piece = pl.ds(c * cb, cb)
                hops[s, c] = send(
                    hop.at[s, piece], hopr.at[s, piece], rsz_sem, s * chunks + c + 1, "week", ahead
                )

        def own_block(b, c):
            own[b] = gathered(mw * nb + b) + dp_s[b]
            return c

        lax.fori_loop(0, nb, own_block, 0)
        finish(paw_copies)
        alpha = from_row(rz_row / jnp.sum(paw[...], axis=0))

        def advance(b, c):
            x_s[b] = x_s[b] + alpha * p_s[b]
            return c

        lax.fori_loop(0, nb, advance, 0)
        def update(b, c):
            image = own[b] + hopr[lines - 2, b].astype(jnp.float32)
            for j in range(rows - 1):
                image = image + rsr[j, lines - 1, b].astype(jnp.float32)
            r_s[b] = r_s[b] - alpha * image
            return c

        for c in range(chunks):
            for j in range(rows - 1):
                aside[j, lines - 1, c].wait_recv()
            hops[lines - 2, c].wait_recv()
            lax.fori_loop(c * cb, (c + 1) * cb, update, 0)
        for copy in list(aside.values()) + list(hops.values()):
            copy.wait_send()
        return carry

    lax.fori_loop(0, ITERS, iteration, 0)
    for b in range(nb):
        x_out[:, b * width:(b + 1) * width] = x_s[b]
        r_out[:, b * width:(b + 1) * width] = r_s[b]


def per_device(nw, ns, right_side, jacobians, week_blocks, block_kind, diagonal_table, precond_table):
    rhs, _, own_length = right_side.shape
    weeks, rank, columns = jacobians.shape
    kb = week_blocks.shape[1]
    width = columns // kb
    nb = own_length // width
    blocks = nb * nw
    wpg = weeks // ns
    rows = 1
    while 4 * rows * rows <= nw:
        rows *= 2
    lines = nw // rows
    chunks = min(CHUNKS, nb)
    slots = 1 + jnp.arange(weeks * kb, dtype=jnp.int32).reshape(weeks, kb)
    numbers = jnp.arange(blocks, dtype=jnp.int32)
    inverse = jnp.sum(
        jnp.where(week_blocks[None] == numbers[:, None, None], slots[None], 0), axis=2
    ).reshape(-1)
    f32, bf16 = jnp.float32, jnp.bfloat16
    smem = pl.BlockSpec(memory_space=pltpu.SMEM)
    vmem = pl.BlockSpec(memory_space=pltpu.VMEM)
    own_state = pltpu.VMEM((nb, rhs, width), f32)

    def sems(count):
        return pltpu.SemaphoreType.DMA((2, count - 1))

    solution, residual = pl.pallas_call(
        functools.partial(kernel, nw, ns, rows, chunks),
        out_shape=[jax.ShapeDtypeStruct((rhs, own_length), f32)] * 2,
        in_specs=[smem] * 3 + [vmem, pl.BlockSpec(memory_space=pl.ANY), vmem, vmem],
        out_specs=[vmem] * 2,
        scratch_shapes=[
            pltpu.VMEM(jacobians.shape, jacobians.dtype),
            pltpu.SemaphoreType.DMA,
            pltpu.VMEM((blocks, rhs, width), bf16),
            pltpu.VMEM((weeks, rhs, rank), bf16),
            pltpu.VMEM((ns - 1, wpg, rhs, rank), bf16),
            pltpu.VMEM((wpg, rhs, rank), f32),
            pltpu.VMEM((wpg, rhs, rank), f32),
            pltpu.VMEM((weeks, rhs, rank), bf16),
            pltpu.VMEM((1 + weeks * kb, rhs, width), f32),
            pltpu.VMEM((rows - 1, lines, nb, rhs, width), bf16),
            pltpu.VMEM((rows - 1, lines, nb, rhs, width), bf16),
            pltpu.VMEM((lines - 1, nb, rhs, width), bf16),
            pltpu.VMEM((lines - 1, nb, rhs, width), bf16),
            own_state, own_state, own_state, own_state, own_state, own_state, own_state,
            pltpu.VMEM((LANES, LANES), f32),
            pltpu.VMEM((1, LANES), f32),
            pltpu.VMEM((nw, 1, LANES), f32),
            pltpu.VMEM((ns, 1, LANES), f32),
            pltpu.VMEM((nw, 1, LANES), f32),
            pltpu.VMEM((ns, 1, LANES), f32),
            sems((lines - 1) * chunks + 1), sems((rows - 1) * lines * chunks + 1),
            sems((rows - 1) * (lines - 1) * max(chunks // 8, 1) + 1),
            sems(ns), sems(ns),
            sems((lines - 1) * chunks + 1), sems((rows - 1) * lines * chunks + 1),
            sems(nw), sems(ns), sems(nw), sems(ns),
        ],
        compiler_params=pltpu.CompilerParams(
            collective_id=0, has_side_effects=True, vmem_limit_bytes=48 * 1024 * 1024
        ),
    )(
        week_blocks.reshape(-1), inverse, block_kind.reshape(-1), right_side[:, 0, :],
        jacobians, diagonal_table, precond_table,
    )
    return (solution[:, None, :], residual[:, None, :])


def solution(mesh):
    placed = (
        P(None, "seg", "week"),
        P("week", None, "seg"),
        P("week", "seg"),
        P("seg", "week"),
        P(),
        P(),
    )
    return jax.shard_map(
        functools.partial(per_device, mesh.shape["week"], mesh.shape["seg"]),
        mesh=mesh,
        in_specs=placed,
        out_specs=(P(None, "seg", "week"), P(None, "seg", "week")),
        check_vma=False,
    )
```
